32 devices in a mesh: section: 8 (over z, x), tensor: 4 (over y, core).
Axes of the slice: x: 2, y: 2, z: 4, core: 2. Of those that a mesh axis runs over, the one named last changes fastest.
Arguments:
- layer_input: bfloat16 [1024, 8192], P('section'), may hold values from -36 to 36
- norm_gain: float32 [8192], replicated, may hold values from 0.5 to 1.5
- kv_weight: bfloat16 [8192, 2048], P('section', 'tensor'), may hold values from -0.0625 to 0.0625
- kv_cotangent: bfloat16 [1024, 2048], P('section', 'tensor'), may hold values from -4 to 4
Outputs:
- weight_grad: float32 [8192, 2048], P('section', 'tensor')
- input_grad: bfloat16 [1024, 8192], P('section')
The draws below stay inside these ranges and needn't reach their ends.
All inputs are finite; a program needn't handle non-finite values.
Results may differ from the reference program's by a relative error of at most 0.0029.
Values may be sent and summed in bfloat16 or wider, within the bound.
A program may use at most 64 MiB of HBM per device.

```python
import math
import jax
import jax.numpy as jnp
from jax import lax

D = 8192
KV = 2048
TOKENS = 1024


def draw_layer_input(key, part):
    key_noise, key_rows, key_cols = jax.random.split(key, 3)
    lower_log = math.log(0.3)
    upper_log = math.log(3.0)
    row_scale = jnp.exp(jax.random.uniform(key_rows, (TOKENS, 1), jnp.float32, lower_log, upper_log))
    col_scale = jnp.exp(jax.random.uniform(key_cols, (1, D), jnp.float32, lower_log, upper_log))
    noise = jnp.clip(jax.random.normal(key_noise, (TOKENS, D), jnp.float32), -4.0, 4.0)
    return (noise * row_scale * col_scale).astype(jnp.bfloat16)


def levels(rng, extent, cuts, smallest, top_value):
    factor_of, own = 1.0, jax.random.fold_in(rng, 6)
    for axis_at, parts in cuts:
        steps = jnp.exp(jax.random.uniform(jax.random.fold_in(own, axis_at), (parts,), jnp.float32, smallest / len(cuts), top_value / len(cuts)))
        factor_of = factor_of * jnp.repeat(steps, extent[axis_at] // parts).reshape([-1 if axis == axis_at else 1 for axis in range(len(extent))])
    return factor_of


def bell_draw(stream_key, extent, deviation, bound, pieces=(), kind=jnp.bfloat16):
    result = jax.random.normal(stream_key, extent, jnp.float32) * deviation
    if len(pieces) > 0:
        result = levels(stream_key, extent, pieces, -0.22, 0.18) * result
    return jnp.clip(result, min=-bound, max=bound).astype(kind)


def setup_inputs(seed: int = 0) -> dict:
    keys = jax.random.split(jax.random.key(seed), 5)
    layer_input = draw_layer_input(jax.random.fold_in(keys[4], 71), 0)
    norm_gain = jnp.clip(1.0 + 0.1 * jax.random.normal(keys[1], (D,), jnp.float32), 0.5, 1.5)
    kv_weight = bell_draw(keys[2], (D, KV), D ** -0.5, 0.0625, ((0, 8), (1, 4)))
    kv_cotangent = bell_draw(keys[3], (TOKENS, KV), 0.25, 4.0, ((0, 8), (1, 4)))
    return {"layer_input": layer_input, "norm_gain": norm_gain, "kv_weight": kv_weight, "kv_cotangent": kv_cotangent}


def reference(layer_input, norm_gain, kv_weight, kv_cotangent):
    hidden = layer_input.astype(jnp.float32)
    inv_rms = lax.rsqrt(lax.optimization_barrier(jnp.mean(hidden * hidden, axis=1, keepdims=True)) + 1e-05)
    unit_rows = hidden * inv_rms
    normed = (unit_rows * norm_gain).astype(jnp.bfloat16)
    weight_grad = jnp.dot(normed.T, kv_cotangent, preferred_element_type=jnp.float32)
    normed_grad = jnp.dot(kv_cotangent, kv_weight.T, preferred_element_type=jnp.float32)
    scaled_grad = norm_gain * normed_grad
    along_unit = lax.optimization_barrier(jnp.mean(scaled_grad * unit_rows, axis=1, keepdims=True))
    input_grad = (inv_rms * (scaled_grad - unit_rows * along_unit)).astype(jnp.bfloat16)
    return (weight_grad, input_grad)
```

```python
import jax
import jax.numpy as jnp
from jax import lax
from jax.sharding import PartitionSpec as P


def per_device(layer_input, norm_gain, kv_weight, kv_cotangent):
    hidden = layer_input.astype(jnp.float32)
    width = hidden.shape[1]
    inv_own = lax.rsqrt(jnp.mean(hidden * hidden, axis=1, keepdims=True) + 1e-05)
    slab = lax.all_to_all(layer_input, "section", split_axis=1, concat_axis=0, tiled=True)
    cotangents = lax.all_gather(kv_cotangent, "section", axis=0, tiled=True)
    inv_rms = lax.all_gather(inv_own, "section", axis=0, tiled=True)
    rows, columns = slab.shape
    tensors = lax.axis_size("tensor")
    share = columns // tensors
    start = lax.axis_index("section") * columns
    gain = lax.dynamic_slice_in_dim(norm_gain, start, columns, 0)
    unit = slab.astype(jnp.float32) * inv_rms
    scaled_unit = unit * gain
    part = lax.dot_general(
        cotangents, kv_weight, (((1,), (1,)), ((), ())), preferred_element_type=jnp.float32
    )
    along = lax.psum(jnp.sum(part * scaled_unit, axis=1, keepdims=True), ("section", "tensor")) / width
    weight_grad = lax.dot_general(
        scaled_unit.astype(jnp.bfloat16),
        cotangents,
        (((0,), (0,)), ((), ())),
        preferred_element_type=jnp.float32,
    )
    reduced = lax.psum_scatter(part, "tensor", scatter_dimension=1, tiled=True)
    offset = lax.axis_index("tensor") * share
    gain_share = lax.dynamic_slice_in_dim(gain, offset, share, 0)
    unit_share = lax.dynamic_slice_in_dim(unit, offset, share, 1)
    share_grad = (inv_rms * (gain_share * reduced - unit_share * along)).astype(jnp.bfloat16)
    mine = lax.all_to_all(share_grad, "section", split_axis=0, concat_axis=0, tiled=True)
    sections = lax.axis_size("section")
    tokens = rows // sections
    every = lax.all_gather(mine, "tensor", axis=0, tiled=False)
    every = every.reshape(tensors, sections, tokens, share)
    input_grad = every.transpose(2, 1, 0, 3).reshape(tokens, width)
    return (weight_grad, input_grad)


def solution(mesh):
    return jax.shard_map(
        per_device,
        mesh=mesh,
        in_specs=(P("section", None), P(), P("section", "tensor"), P("section", "tensor")),
        out_specs=(P("section", "tensor"), P("section", None)),
        check_vma=False,
    )
```

```python
import functools

import jax
import jax.numpy as jnp
from jax import lax
from jax.experimental import pallas as pl
from jax.experimental.pallas import tpu as pltpu
from jax.sharding import PartitionSpec as P

MESH = pl.DeviceIdType.MESH
F32 = jnp.float32
BF16 = jnp.bfloat16
NT = (((1,), (1,)), ((), ()))
TN = (((0,), (0,)), ((), ()))


def kernel(S, T, x, gain, w, dyin, wg, out, invs, invcol, colbuf, dy, dym, wm, xo, xm, nrm, part,
           prcv, albuf, agbuf, alf, fin, inv_s, inv_r, dy_s, dy_r, dm_s, dm_r, wm_s, wm_r, x_s, x_r,
           xm_s, xm_r, p_s, p_r, al_s, al_r, ag_s, ag_r, o_s, o_r, oy_s, oy_r, oc_s, oc_r):
    s = lax.axis_index("section")
    t = lax.axis_index("tensor")
    c = t % 2
    g = t // 2
    G = T // 2
    mate = g * 2 + 1 - c
    tok, width = x.shape
    feats = w.shape[0]
    hf = feats // 2
    R = tok // G

    def copy(src, dst, ss, rs, sec, ten):
        return pltpu.make_async_remote_copy(
            src_ref=src, dst_ref=dst, send_sem=ss, recv_sem=rs,
            device_id={"section": sec, "tensor": ten}, device_id_type=MESH,
        )

    def loop(lo, hi, f):
        def body(k, carry):
            f(k)
            return carry
        lax.fori_loop(lo, hi, body, 0)

    def peer(k):
        return (s + k) % S

    def source(k):
        return (s + S - k) % S

    def other(d):
        return (g + d) % G

    def origin(d):
        return (g + G - d) % G

    def fcols(sec, half):
        return pl.ds(pl.multiple_of(sec * feats + half * hf, hf), hf)

    def rows(gg):
        return pl.ds(pl.multiple_of(gg * R, R), R)

    barrier = pltpu.get_barrier_semaphore()

    def hello(sec, ten):
        pl.semaphore_signal(barrier, inc=1, device_id={"section": sec, "tensor": ten}, device_id_type=MESH)

    def greet(k):
        hello(peer(k), t)
        hello(peer(k), mate)
    loop(1, S, greet)
    hello(s, mate)
    loop(1, G, lambda d: hello(s, other(d) * 2 + c))

    def squares(i, acc):
        v = x[:, pl.ds(pl.multiple_of(i * feats, feats), feats)].astype(F32)
        return acc + jnp.sum(v * v, axis=1, keepdims=True)
    total = lax.fori_loop(0, width // feats, squares, jnp.zeros((tok, 1), F32))
    inv_own = lax.rsqrt(total / width + 1e-05)
    invs[s] = jnp.transpose(jnp.broadcast_to(inv_own, (tok, 128)))[0:8]
    pl.semaphore_wait(barrier, 2 * S - 1 + G - 1)

    def wm_copy():
        half = pl.ds(pl.multiple_of((1 - c) * hf, hf), hf)
        return copy(w.at[half], wm, wm_s.at[0], wm_r.at[0], s, mate)

    def dy_copy(k):
        return copy(dyin, dy.at[s], dy_s.at[k], dy_r.at[k], peer(k), t)

    def inv_copy(k):
        return copy(invs.at[s], invs.at[s], inv_s.at[k], inv_r.at[k], peer(k), t)

    def x_copy(k):
        return copy(x.at[:, fcols(peer(k), c)], xo.at[s], x_s.at[k], x_r.at[k], peer(k), t)

    def dm_copy(k):
        return copy(dy.at[source(k)], dym.at[source(k)], dm_s.at[k], dm_r.at[k], s, mate)

    def dm_own():
        return copy(dyin, dym.at[s], dm_s.at[0], dm_r.at[0], s, mate)

    def xm_copy(k):
        return copy(xo.at[source(k)], xm.at[source(k)], xm_s.at[k], xm_r.at[k], s, mate)

    wm_copy().start()
    dm_own().start()
    loop(1, S, lambda k: dy_copy(k).start())
    loop(1, S, lambda k: inv_copy(k).start())
    loop(1, S, lambda k: x_copy(k).start())
    dy[s] = dyin[...]
    xo[s] = x[:, fcols(s, c)]
    xm[s] = x[:, fcols(s, 1 - c)]

    wm_copy().wait_recv()
    own_half = pl.ds(pl.multiple_of(c * hf, hf), hf)

    def p_copy(k, d):
        sec = source(k)
        i = k * G + d
        return copy(part.at[sec, rows(other(d))], prcv.at[d, sec], p_s.at[i], p_r.at[i], s, other(d) * 2 + c)

    def multiply(k):
        sec = source(k)
        dm_copy(k).wait_recv()
        part[sec] = lax.dot_general(dy[sec], w[own_half, :], NT, preferred_element_type=F32) + lax.dot_general(
            dym[sec], wm[...], NT, preferred_element_type=F32)

    def pass_cotangent(k):
        copy(dyin, dy.at[source(k)], dy_s.at[k], dy_r.at[k], peer(k), t).wait_recv()
        dm_copy(k).start()

    def send_part(k):
        loop(1, G, lambda d: p_copy(k, d).start())

    def stage(k):
        pass_cotangent(k)
        multiply(k - 1)
        send_part(k - 1)
    loop(1, S, stage)
    multiply(S - 1)
    send_part(S - 1)

    lanes = lax.broadcasted_iota(jnp.int32, (S, tok), 0)

    def unit_block(k, acc):
        sec = source(k)
        col = jnp.transpose(jnp.broadcast_to(invs[sec][0:1], (128, tok)))
        invcol[sec] = col
        unit = xo[sec].astype(F32) * col[:, 0:1]
        scaled = unit * gain[:, fcols(s, c)]
        nrm[pl.ds(pl.multiple_of(sec * tok, tok), tok), :] = scaled.astype(BF16)
        sums = jnp.sum(scaled * part[sec], axis=1, keepdims=True)
        row = jnp.transpose(jnp.broadcast_to(sums, (tok, 128)))[0:1]
        return jnp.where(lanes == sec, jnp.broadcast_to(row, (S, tok)), acc)

    def token_block(k, acc):
        sec = source(k)
        copy(invs.at[s], invs.at[sec], inv_s.at[k], inv_r.at[k], peer(k), t).wait_recv()
        copy(xo.at[s], xo.at[sec], x_s.at[k], x_r.at[k], peer(k), t).wait_recv()
        xm_copy(k).start()
        return unit_block(k, acc)
    along = unit_block(0, jnp.zeros((S, tok), F32))
    along = lax.fori_loop(1, S, token_block, along)
    albuf[0, 0] = along

    def al_copy(k, m):
        return copy(albuf.at[0, 0], albuf.at[k, m], al_s.at[k * 2 + m], al_r.at[k * 2 + m], peer(k),
                    t if m == 0 else mate)

    def al_send(k):
        al_copy(k, 0).start()
        al_copy(k, 1).start()
    al_copy(0, 1).start()
    loop(1, S, al_send)

    def weight_half(half):
        flat = dy[...].reshape(S * tok, dyin.shape[1])
        wg[pl.ds(pl.multiple_of(half * hf, hf), hf), :] = lax.dot_general(
            nrm[...], flat, TN, preferred_element_type=F32)
    weight_half(c)

    al_copy(0, 1).wait_recv()

    def al_wait(k, acc):
        al_copy(k, 0).wait_recv()
        al_copy(k, 1).wait_recv()
        return acc + (albuf[k, 0] + albuf[k, 1])
    along = lax.fori_loop(1, S, al_wait, albuf[0, 0] + albuf[0, 1])
    agbuf[0] = along

    def ag_copy(d):
        return copy(agbuf.at[0], agbuf.at[d], ag_s.at[d], ag_r.at[d], s, other(d) * 2 + c)
    loop(1, G, lambda d: ag_copy(d).start())

    def ag_wait(d, acc):
        ag_copy(d).wait_recv()
        return acc + agbuf[d]

    def p_wait(k):
        loop(1, G, lambda d: p_copy(k, d).wait_recv())
    loop(0, S, p_wait)
    alf[...] = lax.fori_loop(1, G, ag_wait, along) / width

    def finish(sec):
        def add(d, acc):
            return acc + prcv[d, sec]
        reduced = lax.fori_loop(1, G, add, part[sec, rows(g), :])
        colbuf[...] = jnp.transpose(jnp.broadcast_to(alf[pl.ds(sec, 1), :], (128, tok)))
        inv = invcol[sec, rows(g), :][:, 0:1]
        al = colbuf[rows(g), :][:, 0:1]
        unit = xo[sec, rows(g), :].astype(F32) * inv
        return (inv * (gain[:, fcols(s, c)] * reduced - unit * al)).astype(BF16)

    def region(sec, gg, half):
        return out.at[rows(gg), fcols(sec, half)]

    def o_copy(k):
        return copy(fin.at[peer(k)], region(s, g, c), o_s.at[k], o_r.at[k], peer(k), t)

    def oy_copy(k, d):
        place = region(source(k), g, c)
        return copy(place, place, oy_s.at[k * G + d], oy_r.at[k * G + d], s, other(d) * 2 + c)

    def oc_copy(k, d):
        place = region(source(k), origin(d), c)
        return copy(place, place, oc_s.at[k * G + d], oc_r.at[k * G + d], s, mate)

    def send_on(k):
        loop(1, G, lambda d: oy_copy(k, d).start())
        oc_copy(k, 0).start()

    def send_rows(k):
        fin[peer(k)] = finish(peer(k))
        o_copy(k).start()
    loop(1, S, send_rows)
    out[rows(g), fcols(s, c)] = finish(s)
    send_on(0)

    def mate_block(k):
        sec = source(k)
        unit = xm[sec].astype(F32) * invcol[sec][:, 0:1]
        scaled = unit * gain[:, fcols(s, 1 - c)]
        nrm[pl.ds(pl.multiple_of(sec * tok, tok), tok), :] = scaled.astype(BF16)

    def mate_wait(k):
        xm_copy(k).wait_recv()
        mate_block(k)
    mate_block(0)
    loop(1, S, mate_wait)
    weight_half(1 - c)

    def arrive(k):
        place = region(source(k), g, c)
        copy(place, place, o_s.at[k], o_r.at[k], peer(k), t).wait_recv()
        send_on(k)
    loop(1, S, arrive)

    def arrive_y(k):
        def one(d):
            place = region(source(k), origin(d), c)
            copy(place, place, oy_s.at[k * G + d], oy_r.at[k * G + d], s, mate).wait_recv()
            oc_copy(k, d).start()
        loop(1, G, one)
    loop(0, S, arrive_y)

    def arrive_mate(k):
        def one(d):
            place = region(source(k), origin(d), 1 - c)
            copy(place, place, oc_s.at[k * G + d], oc_r.at[k * G + d], s, mate).wait_recv()
        loop(0, G, one)
    loop(0, S, arrive_mate)

    wm_copy().wait_send()
    dm_own().wait_send()
    al_copy(0, 1).wait_send()
    loop(1, G, lambda d: ag_copy(d).wait_send())

    def drain(k):
        dy_copy(k).wait_send()
        inv_copy(k).wait_send()
        x_copy(k).wait_send()
        dm_copy(k).wait_send()
        xm_copy(k).wait_send()
        al_copy(k, 0).wait_send()
        al_copy(k, 1).wait_send()
        o_copy(k).wait_send()
    loop(1, S, drain)

    def drain_all(k):
        def one(d):
            p_copy(k, d).wait_send()
            oy_copy(k, d).wait_send()
            oc_copy(k, d).wait_send()
        loop(1, G, one)
        oc_copy(k, 0).wait_send()
    loop(0, S, drain_all)


def solution(mesh):
    S, T = mesh.shape["section"], mesh.shape["tensor"]
    G = T // 2

    def per_device(layer_input, norm_gain, kv_weight, kv_cotangent):
        tok, width = layer_input.shape
        feats, cols = kv_weight.shape
        hf, R = feats // 2, tok // G
        dma = pltpu.SemaphoreType.DMA
        vmem = pl.BlockSpec(memory_space=pltpu.VMEM)
        V = pltpu.VMEM
        return tuple(pl.pallas_call(
            functools.partial(kernel, S, T),
            out_shape=(jax.ShapeDtypeStruct((feats, cols), F32), jax.ShapeDtypeStruct((tok, width), BF16)),
            in_specs=[vmem] * 4,
            out_specs=(vmem, vmem),
            scratch_shapes=[
                V((S, 8, tok), F32), V((S, tok, 128), F32), V((tok, 128), F32),
                V((S, tok, cols), BF16), V((S, tok, cols), BF16), V((hf, cols), BF16),
                V((S, tok, hf), BF16), V((S, tok, hf), BF16), V((S * tok, hf), BF16),
                V((S, tok, hf), F32), V((G, S, R, hf), F32),
                V((S, 2, S, tok), F32), V((G, S, tok), F32), V((S, tok), F32), V((S, R, hf), BF16),
                dma((S,)), dma((S,)), dma((S,)), dma((S,)), dma((S,)), dma((S,)), dma((1,)), dma((1,)),
                dma((S,)), dma((S,)), dma((S,)), dma((S,)), dma((S * G,)), dma((S * G,)),
                dma((S * 2,)), dma((S * 2,)), dma((G,)), dma((G,)), dma((S,)), dma((S,)),
                dma((S * G,)), dma((S * G,)), dma((S * G,)), dma((S * G,)),
            ],
            compiler_params=pltpu.CompilerParams(
                collective_id=0, has_side_effects=True, vmem_limit_bytes=56 * 1024 * 1024),
        )(layer_input, norm_gain.reshape(1, width), kv_weight, kv_cotangent))

    return jax.shard_map(
        per_device,
        mesh=mesh,
        in_specs=(P("section", None), P(), P("section", "tensor"), P("section", "tensor")),
        out_specs=(P("section", "tensor"), P("section", None)),
        check_vma=False,
    )
```

```python
import functools

import jax
import jax.numpy as jnp
from jax import lax
from jax.experimental import pallas as pl
from jax.experimental.pallas import tpu as pltpu
from jax.sharding import PartitionSpec as P

MESH = pl.DeviceIdType.MESH
F32 = jnp.float32
BF16 = jnp.bfloat16
NT = (((1,), (1,)), ((), ()))
TN = (((0,), (0,)), ((), ()))


def kernel(S, T, x, gain, w, dyin, wg, out, invs, invcol, colbuf, dy, dym, wm, xo, xm, nrm, part,
           prcv, albuf, agbuf, alf, fin, inv_s, inv_r, dy_s, dy_r, dm_s, dm_r, wm_s, wm_r, x_s, x_r,
           xm_s, xm_r, p_s, p_r, al_s, al_r, ag_s, ag_r, o_s, o_r, oy_s, oy_r, oc_s, oc_r):
    s = lax.axis_index("section")
    t = lax.axis_index("tensor")
    c = t % 2
    g = t // 2
    G = T // 2
    Z = S // 2
    mate = g * 2 + 1 - c
    tok, width = x.shape
    feats = w.shape[0]
    hf = feats // 2
    R = tok // G

    def copy(src, dst, ss, rs, sec, ten):
        return pltpu.make_async_remote_copy(
            src_ref=src, dst_ref=dst, send_sem=ss, recv_sem=rs,
            device_id={"section": sec, "tensor": ten}, device_id_type=MESH,
        )

    def loop(lo, hi, f):
        def body(k, carry):
            f(k)
            return carry
        lax.fori_loop(lo, hi, body, 0)

    def peer(k):
        return (s // 2 + k // 2) % Z * 2 + (s + k) % 2

    def source(k):
        return (s // 2 + Z - k // 2) % Z * 2 + (s + k) % 2

    def other(d):
        return (g + d) % G

    def origin(d):
        return (g + G - d) % G

    def fcols(sec, half):
        return pl.ds(pl.multiple_of(sec * feats + half * hf, hf), hf)

    def rows(gg):
        return pl.ds(pl.multiple_of(gg * R, R), R)

    barrier = pltpu.get_barrier_semaphore()

    def hello(sec, ten):
        pl.semaphore_signal(barrier, inc=1, device_id={"section": sec, "tensor": ten}, device_id_type=MESH)

    def greet(k):
        hello(peer(k), t)
        hello(peer(k), mate)
    loop(1, S, greet)
    hello(s, mate)
    loop(1, G, lambda d: hello(s, other(d) * 2 + c))

    def squares(i, acc):
        v = x[:, pl.ds(pl.multiple_of(i * feats, feats), feats)].astype(F32)
        return acc + jnp.sum(v * v, axis=1, keepdims=True)
    total = lax.fori_loop(0, width // feats, squares, jnp.zeros((tok, 1), F32))
    inv_own = lax.rsqrt(total / width + 1e-05)
    invs[s] = jnp.transpose(jnp.broadcast_to(inv_own, (tok, 128)))[0:8]
    pl.semaphore_wait(barrier, 2 * S - 1 + G - 1)

    def wm_copy():
        half = pl.ds(pl.multiple_of((1 - c) * hf, hf), hf)
        return copy(w.at[half], wm, wm_s.at[0], wm_r.at[0], s, mate)

    def dy_copy(k):
        return copy(dyin, dy.at[s], dy_s.at[k], dy_r.at[k], peer(k), t)

    def inv_copy(k):
        return copy(invs.at[s], invs.at[s], inv_s.at[k], inv_r.at[k], peer(k), t)

    def x_copy(k):
        return copy(x.at[:, fcols(peer(k), c)], xo.at[s], x_s.at[k], x_r.at[k], peer(k), t)

    def dm_copy(k):
        return copy(dy.at[source(k)], dym.at[source(k)], dm_s.at[k], dm_r.at[k], s, mate)

    def dm_own():
        return copy(dyin, dym.at[s], dm_s.at[0], dm_r.at[0], s, mate)

    def xm_copy(k):
        return copy(xo.at[source(k)], xm.at[source(k)], xm_s.at[k], xm_r.at[k], s, mate)

    wm_copy().start()
    dm_own().start()
    dy_copy(1).start()
    loop(1, Z, lambda i: dy_copy(2 * i).start())
    loop(1, S, lambda k: inv_copy(k).start())
    loop(1, Z, lambda i: x_copy(2 * i).start())
    dy[s] = dyin[...]
    xo[s] = x[:, fcols(s, c)]
    xm[s] = x[:, fcols(s, 1 - c)]

    wm_copy().wait_recv()
    own_half = pl.ds(pl.multiple_of(c * hf, hf), hf)

    def p_copy(k, d):
        sec = source(k)
        i = k * G + d
        return copy(part.at[sec, rows(other(d))], prcv.at[d, sec], p_s.at[i], p_r.at[i], s, other(d) * 2 + c)

    def multiply(k):
        sec = source(k)
        dm_copy(k).wait_recv()
        part[sec] = lax.dot_general(dy[sec], w[own_half, :], NT, preferred_element_type=F32) + lax.dot_general(
            dym[sec], wm[...], NT, preferred_element_type=F32)

    def pass_cotangent(k):
        copy(dyin, dy.at[source(k)], dy_s.at[k], dy_r.at[k], peer(k), t).wait_recv()
        dm_copy(k).start()

    def relay(k):
        return copy(dy.at[source(k)], dy.at[source(k)], dy_s.at[k + 1], dy_r.at[k + 1], peer(1), t)

    def pass_relay(k):
        pass_cotangent(k)
        relay(k).start()

    def use(k):
        multiply(k)
        loop(1, G, lambda d: p_copy(k, d).start())

    pass_cotangent(1)
    use(0)
    pass_relay(2)
    use(1)

    def even(i):
        pass_relay(2 * i)
        use(2 * i - 2)
    loop(2, Z, even)
    loop(0, Z, lambda i: x_copy(2 * i + 1).start())
    use(2 * Z - 2)
    pass_cotangent(3)

    def odd(i):
        pass_cotangent(2 * i + 1)
        use(2 * i - 1)
    loop(2, Z, odd)
    use(2 * Z - 1)

    lanes = lax.broadcasted_iota(jnp.int32, (S, tok), 0)

    def unit_block(k, acc):
        sec = source(k)
        col = jnp.transpose(jnp.broadcast_to(invs[sec][0:1], (128, tok)))
        invcol[sec] = col
        unit = xo[sec].astype(F32) * col[:, 0:1]
        scaled = unit * gain[:, fcols(s, c)]
        nrm[pl.ds(pl.multiple_of(sec * tok, tok), tok), :] = scaled.astype(BF16)
        sums = jnp.sum(scaled * part[sec], axis=1, keepdims=True)
        row = jnp.transpose(jnp.broadcast_to(sums, (tok, 128)))[0:1]
        return jnp.where(lanes == sec, jnp.broadcast_to(row, (S, tok)), acc)

    def token_block(k, acc):
        sec = source(k)
        copy(invs.at[s], invs.at[sec], inv_s.at[k], inv_r.at[k], peer(k), t).wait_recv()
        copy(xo.at[s], xo.at[sec], x_s.at[k], x_r.at[k], peer(k), t).wait_recv()
        xm_copy(k).start()
        return unit_block(k, acc)
    along = unit_block(0, jnp.zeros((S, tok), F32))
    along = lax.fori_loop(1, Z, lambda i, acc: token_block(2 * i, acc), along)
    along = lax.fori_loop(0, Z, lambda i, acc: token_block(2 * i + 1, acc), along)
    albuf[0, 0] = along

    def al_copy(k, m):
        return copy(albuf.at[0, 0], albuf.at[k, m], al_s.at[k * 2 + m], al_r.at[k * 2 + m], peer(k),
                    t if m == 0 else mate)

    def al_send(k):
        al_copy(k, 0).start()
        al_copy(k, 1).start()
    al_copy(0, 1).start()
    loop(1, S, al_send)

    def weight_half(half):
        flat = dy[...].reshape(S * tok, dyin.shape[1])
        wg[pl.ds(pl.multiple_of(half * hf, hf), hf), :] = lax.dot_general(
            nrm[...], flat, TN, preferred_element_type=F32)
    weight_half(c)

    al_copy(0, 1).wait_recv()

    def al_wait(k, acc):
        al_copy(k, 0).wait_recv()
        al_copy(k, 1).wait_recv()
        return acc + (albuf[k, 0] + albuf[k, 1])
    along = lax.fori_loop(1, S, al_wait, albuf[0, 0] + albuf[0, 1])
    agbuf[0] = along

    def ag_copy(d):
        return copy(agbuf.at[0], agbuf.at[d], ag_s.at[d], ag_r.at[d], s, other(d) * 2 + c)
    loop(1, G, lambda d: ag_copy(d).start())

    def ag_wait(d, acc):
        ag_copy(d).wait_recv()
        return acc + agbuf[d]

    def p_wait(k):
        loop(1, G, lambda d: p_copy(k, d).wait_recv())
    loop(0, S, p_wait)
    alf[...] = lax.fori_loop(1, G, ag_wait, along) / width

    def finish(sec):
        def add(d, acc):
            return acc + prcv[d, sec]
        reduced = lax.fori_loop(1, G, add, part[sec, rows(g), :])
        colbuf[...] = jnp.transpose(jnp.broadcast_to(alf[pl.ds(sec, 1), :], (128, tok)))
        inv = invcol[sec, rows(g), :][:, 0:1]
        al = colbuf[rows(g), :][:, 0:1]
        unit = xo[sec, rows(g), :].astype(F32) * inv
        return (inv * (gain[:, fcols(s, c)] * reduced - unit * al)).astype(BF16)

    def region(sec, gg, half):
        return out.at[rows(gg), fcols(sec, half)]

    def o_copy(k):
        return copy(fin.at[peer(k)], region(s, g, c), o_s.at[k], o_r.at[k], peer(k), t)

    def oy_copy(k, d):
        place = region(source(k), g, c)
        return copy(place, place, oy_s.at[k * G + d], oy_r.at[k * G + d], s, other(d) * 2 + c)

    def oc_copy(k, d):
        place = region(source(k), origin(d), c)
        return copy(place, place, oc_s.at[k * G + d], oc_r.at[k * G + d], s, mate)

    def send_on(k):
        loop(1, G, lambda d: oy_copy(k, d).start())
        oc_copy(k, 0).start()

    def send_rows(k):
        fin[peer(k)] = finish(peer(k))
        o_copy(k).start()
    loop(1, S, send_rows)
    out[rows(g), fcols(s, c)] = finish(s)
    send_on(0)

    def mate_block(k):
        sec = source(k)
        unit = xm[sec].astype(F32) * invcol[sec][:, 0:1]
        scaled = unit * gain[:, fcols(s, 1 - c)]
        nrm[pl.ds(pl.multiple_of(sec * tok, tok), tok), :] = scaled.astype(BF16)

    def mate_wait(k):
        xm_copy(k).wait_recv()
        mate_block(k)
    mate_block(0)
    loop(1, S, mate_wait)
    weight_half(1 - c)

    def arrive(k):
        place = region(source(k), g, c)
        copy(place, place, o_s.at[k], o_r.at[k], peer(k), t).wait_recv()
        send_on(k)
    loop(1, S, arrive)

    def arrive_y(k):
        def one(d):
            place = region(source(k), origin(d), c)
            copy(place, place, oy_s.at[k * G + d], oy_r.at[k * G + d], s, mate).wait_recv()
            oc_copy(k, d).start()
        loop(1, G, one)
    loop(0, S, arrive_y)

    def arrive_mate(k):
        def one(d):
            place = region(source(k), origin(d), 1 - c)
            copy(place, place, oc_s.at[k * G + d], oc_r.at[k * G + d], s, mate).wait_recv()
        loop(0, G, one)
    loop(0, S, arrive_mate)

    wm_copy().wait_send()
    dm_own().wait_send()
    al_copy(0, 1).wait_send()
    loop(1, G, lambda d: ag_copy(d).wait_send())

    def drain(k):
        inv_copy(k).wait_send()
        x_copy(k).wait_send()
        dm_copy(k).wait_send()
        xm_copy(k).wait_send()
        al_copy(k, 0).wait_send()
        al_copy(k, 1).wait_send()
        o_copy(k).wait_send()
    loop(1, S, drain)
    dy_copy(1).wait_send()

    def drain_dy(i):
        dy_copy(2 * i).wait_send()
        relay(2 * i).wait_send()
    loop(1, Z, drain_dy)

    def drain_all(k):
        def one(d):
            p_copy(k, d).wait_send()
            oy_copy(k, d).wait_send()
            oc_copy(k, d).wait_send()
        loop(1, G, one)
        oc_copy(k, 0).wait_send()
    loop(0, S, drain_all)


def solution(mesh):
    S, T = mesh.shape["section"], mesh.shape["tensor"]
    G = T // 2

    def per_device(layer_input, norm_gain, kv_weight, kv_cotangent):
        tok, width = layer_input.shape
        feats, cols = kv_weight.shape
        hf, R = feats // 2, tok // G
        dma = pltpu.SemaphoreType.DMA
        vmem = pl.BlockSpec(memory_space=pltpu.VMEM)
        V = pltpu.VMEM
        return tuple(pl.pallas_call(
            functools.partial(kernel, S, T),
            out_shape=(jax.ShapeDtypeStruct((feats, cols), F32), jax.ShapeDtypeStruct((tok, width), BF16)),
            in_specs=[vmem] * 4,
            out_specs=(vmem, vmem),
            scratch_shapes=[
                V((S, 8, tok), F32), V((S, tok, 128), F32), V((tok, 128), F32),
                V((S, tok, cols), BF16), V((S, tok, cols), BF16), V((hf, cols), BF16),
                V((S, tok, hf), BF16), V((S, tok, hf), BF16), V((S * tok, hf), BF16),
                V((S, tok, hf), F32), V((G, S, R, hf), F32),
                V((S, 2, S, tok), F32), V((G, S, tok), F32), V((S, tok), F32), V((S, R, hf), BF16),
                dma((S,)), dma((S,)), dma((S,)), dma((S,)), dma((S,)), dma((S,)), dma((1,)), dma((1,)),
                dma((S,)), dma((S,)), dma((S,)), dma((S,)), dma((S * G,)), dma((S * G,)),
                dma((S * 2,)), dma((S * 2,)), dma((G,)), dma((G,)), dma((S,)), dma((S,)),
                dma((S * G,)), dma((S * G,)), dma((S * G,)), dma((S * G,)),
            ],
            compiler_params=pltpu.CompilerParams(
                collective_id=0, has_side_effects=True, vmem_limit_bytes=56 * 1024 * 1024),
        )(layer_input, norm_gain.reshape(1, width), kv_weight, kv_cotangent))

    return jax.shard_map(
        per_device,
        mesh=mesh,
        in_specs=(P("section", None), P(), P("section", "tensor"), P("section", "tensor")),
        out_specs=(P("section", "tensor"), P("section", None)),
        check_vma=False,
    )
```

```python
import functools

import jax
import jax.numpy as jnp
from jax import lax
from jax.experimental import pallas as pl
from jax.experimental.pallas import tpu as pltpu
from jax.sharding import PartitionSpec as P

MESH = pl.DeviceIdType.MESH
F32 = jnp.float32
BF16 = jnp.bfloat16
NT = (((1,), (1,)), ((), ()))
TN = (((0,), (0,)), ((), ()))


def kernel(S, T, x, gain, w, dyin, wg, out, invs, invcol, colbuf, dy, dym, wm, xo, xm, nrm, part,
           prcv, albuf, agbuf, alf, fin, inv_s, inv_r, dy_s, dy_r, dm_s, dm_r, wm_s, wm_r, x_s, x_r,
           xm_s, xm_r, p_s, p_r, al_s, al_r, ag_s, ag_r, o_s, o_r, oy_s, oy_r, oc_s, oc_r):
    s = lax.axis_index("section")
    t = lax.axis_index("tensor")
    c = t % 2
    g = t // 2
    G = T // 2
    Z = S // 2
    mate = g * 2 + 1 - c
    tok, width = x.shape
    feats = w.shape[0]
    hf = feats // 2
    R = tok // G

    def copy(src, dst, ss, rs, sec, ten):
        return pltpu.make_async_remote_copy(
            src_ref=src, dst_ref=dst, send_sem=ss, recv_sem=rs,
            device_id={"section": sec, "tensor": ten}, device_id_type=MESH,
        )

    def loop(lo, hi, f):
        def body(k, carry):
            f(k)
            return carry
        lax.fori_loop(lo, hi, body, 0)

    def peer(k):
        return (s // 2 + k // 2) % Z * 2 + (s + k) % 2

    def source(k):
        return (s // 2 + Z - k // 2) % Z * 2 + (s + k) % 2

    def other(d):
        return (g + d) % G

    def origin(d):
        return (g + G - d) % G

    def fcols(sec, half):
        return pl.ds(pl.multiple_of(sec * feats + half * hf, hf), hf)

    def rows(gg):
        return pl.ds(pl.multiple_of(gg * R, R), R)

    barrier = pltpu.get_barrier_semaphore()

    def hello(sec, ten):
        pl.semaphore_signal(barrier, inc=1, device_id={"section": sec, "tensor": ten}, device_id_type=MESH)

    def greet(k):
        hello(peer(k), t)
        hello(peer(k), mate)
    loop(1, S, greet)
    hello(s, mate)
    loop(1, G, lambda d: hello(s, other(d) * 2 + c))

    def squares(i, acc):
        v = x[:, pl.ds(pl.multiple_of(i * feats, feats), feats)].astype(F32)
        return acc + jnp.sum(v * v, axis=1, keepdims=True)
    total = lax.fori_loop(0, width // feats, squares, jnp.zeros((tok, 1), F32))
    inv_own = lax.rsqrt(total / width + 1e-05)
    invs[s] = jnp.transpose(jnp.broadcast_to(inv_own, (tok, 128)))[0:8]
    pl.semaphore_wait(barrier, 2 * S - 1 + G - 1)

    def wm_copy():
        half = pl.ds(pl.multiple_of((1 - c) * hf, hf), hf)
        return copy(w.at[half], wm, wm_s.at[0], wm_r.at[0], s, mate)

    def dy_copy(k):
        return copy(dyin, dy.at[s], dy_s.at[k], dy_r.at[k], peer(k), t)

    def inv_copy(k):
        return copy(invs.at[s], invs.at[s], inv_s.at[k], inv_r.at[k], peer(k), t)

    def x_copy(k):
        return copy(x.at[:, fcols(peer(k), c)], xo.at[s], x_s.at[k], x_r.at[k], peer(k), t)

    def dm_copy(k):
        return copy(dy.at[source(k)], dym.at[source(k)], dm_s.at[k], dm_r.at[k], s, mate)

    def dm_own():
        return copy(dyin, dym.at[s], dm_s.at[0], dm_r.at[0], s, mate)

    def xm_copy(k):
        return copy(xo.at[source(k)], xm.at[source(k)], xm_s.at[k], xm_r.at[k], s, mate)

    wm_copy().start()
    dm_own().start()
    dy_copy(1).start()
    loop(1, Z, lambda i: dy_copy(2 * i).start())
    loop(1, S, lambda k: inv_copy(k).start())
    loop(1, Z, lambda i: x_copy(2 * i).start())
    dy[s] = dyin[...]
    xo[s] = x[:, fcols(s, c)]
    xm[s] = x[:, fcols(s, 1 - c)]

    wm_copy().wait_recv()
    own_half = pl.ds(pl.multiple_of(c * hf, hf), hf)

    def p_copy(k, d):
        sec = source(k)
        i = k * G + d
        return copy(part.at[sec, rows(other(d))], prcv.at[d, sec], p_s.at[i], p_r.at[i], s, other(d) * 2 + c)

    def multiply(k):
        sec = source(k)
        dm_copy(k).wait_recv()
        part[sec] = lax.dot_general(dy[sec], w[own_half, :], NT, preferred_element_type=F32) + lax.dot_general(
            dym[sec], wm[...], NT, preferred_element_type=F32)

    def pass_cotangent(k):
        copy(dyin, dy.at[source(k)], dy_s.at[k], dy_r.at[k], peer(k), t).wait_recv()
        dm_copy(k).start()

    def relay(k):
        return copy(dy.at[source(k)], dy.at[source(k)], dy_s.at[k + 1], dy_r.at[k + 1], peer(1), t)

    def pass_relay(k):
        pass_cotangent(k)
        relay(k).start()

    def use(k):
        multiply(k)
        loop(1, G, lambda d: p_copy(k, d).start())

    pass_cotangent(1)
    use(0)
    pass_relay(2)
    use(1)

    def even(i):
        pass_relay(2 * i)
        use(2 * i - 2)
    loop(2, Z, even)
    loop(0, Z, lambda i: x_copy(2 * i + 1).start())
    use(2 * Z - 2)
    pass_cotangent(3)

    def odd(i):
        pass_cotangent(2 * i + 1)
        use(2 * i - 1)
    loop(2, Z, odd)
    use(2 * Z - 1)

    lanes = lax.broadcasted_iota(jnp.int32, (S, tok), 0)

    def unit_block(k, acc):
        sec = source(k)
        col = jnp.transpose(jnp.broadcast_to(invs[sec][0:1], (128, tok)))
        invcol[sec] = col
        unit = xo[sec].astype(F32) * col[:, 0:1]
        scaled = unit * gain[:, fcols(s, c)]
        nrm[pl.ds(pl.multiple_of(sec * tok, tok), tok), :] = scaled.astype(BF16)
        sums = jnp.sum(scaled * part[sec], axis=1, keepdims=True)
        row = jnp.transpose(jnp.broadcast_to(sums, (tok, 128)))[0:1]
        return jnp.where(lanes == sec, jnp.broadcast_to(row, (S, tok)), acc)

    def token_block(k, acc):
        sec = source(k)
        copy(invs.at[s], invs.at[sec], inv_s.at[k], inv_r.at[k], peer(k), t).wait_recv()
        copy(xo.at[s], xo.at[sec], x_s.at[k], x_r.at[k], peer(k), t).wait_recv()
        xm_copy(k).start()
        return unit_block(k, acc)

    def grad_block(k, first=False):
        sec = source(k)
        if not first:
            xm_copy(k).wait_recv()
        unit = xm[sec].astype(F32) * invcol[sec][:, 0:1]
        scaled = (unit * gain[:, fcols(s, 1 - c)]).astype(BF16)
        own = nrm[pl.ds(pl.multiple_of(sec * tok, tok), tok), :]
        for half, block in ((c, own), (1 - c, scaled)):
            place = pl.ds(pl.multiple_of(half * hf, hf), hf)
            term = lax.dot_general(block, dy[sec], TN, preferred_element_type=F32)
            wg[place, :] = term if first else wg[place, :] + term

    along = unit_block(0, jnp.zeros((S, tok), F32))
    along = token_block(2, along)
    grad_block(0, True)

    def even_block(i, acc):
        acc = token_block(2 * i, acc)
        grad_block(2 * i - 2)
        return acc

    def odd_block(i, acc):
        acc = token_block(2 * i + 1, acc)
        grad_block(2 * i - 1)
        return acc
    along = lax.fori_loop(2, Z, even_block, along)
    along = token_block(1, along)
    grad_block(2 * Z - 2)
    along = lax.fori_loop(1, Z, odd_block, along)
    albuf[0, 0] = along

    def al_copy(k, m):
        return copy(albuf.at[0, 0], albuf.at[k, m], al_s.at[k * 2 + m], al_r.at[k * 2 + m], peer(k),
                    t if m == 0 else mate)

    def al_send(k):
        al_copy(k, 0).start()
        al_copy(k, 1).start()
    al_copy(0, 1).start()
    loop(1, S, al_send)

    grad_block(2 * Z - 1)

    al_copy(0, 1).wait_recv()

    def al_wait(k, acc):
        al_copy(k, 0).wait_recv()
        al_copy(k, 1).wait_recv()
        return acc + (albuf[k, 0] + albuf[k, 1])
    along = lax.fori_loop(1, S, al_wait, albuf[0, 0] + albuf[0, 1])
    agbuf[0] = along

    def ag_copy(d):
        return copy(agbuf.at[0], agbuf.at[d], ag_s.at[d], ag_r.at[d], s, other(d) * 2 + c)
    loop(1, G, lambda d: ag_copy(d).start())

    def ag_wait(d, acc):
        ag_copy(d).wait_recv()
        return acc + agbuf[d]

    def p_wait(k):
        loop(1, G, lambda d: p_copy(k, d).wait_recv())
    loop(0, S, p_wait)
    alf[...] = lax.fori_loop(1, G, ag_wait, along) / width

    def finish(sec):
        def add(d, acc):
            return acc + prcv[d, sec]
        reduced = lax.fori_loop(1, G, add, part[sec, rows(g), :])
        colbuf[...] = jnp.transpose(jnp.broadcast_to(alf[pl.ds(sec, 1), :], (128, tok)))
        inv = invcol[sec, rows(g), :][:, 0:1]
        al = colbuf[rows(g), :][:, 0:1]
        unit = xo[sec, rows(g), :].astype(F32) * inv
        return (inv * (gain[:, fcols(s, c)] * reduced - unit * al)).astype(BF16)

    def region(sec, gg, half):
        return out.at[rows(gg), fcols(sec, half)]

    def o_copy(k):
        return copy(fin.at[peer(k)], region(s, g, c), o_s.at[k], o_r.at[k], peer(k), t)

    def oy_copy(k, d):
        place = region(source(k), g, c)
        return copy(place, place, oy_s.at[k * G + d], oy_r.at[k * G + d], s, other(d) * 2 + c)

    def oc_copy(k, d):
        place = region(source(k), origin(d), c)
        return copy(place, place, oc_s.at[k * G + d], oc_r.at[k * G + d], s, mate)

    def send_on(k):
        loop(1, G, lambda d: oy_copy(k, d).start())
        oc_copy(k, 0).start()

    def send_rows(k):
        fin[peer(k)] = finish(peer(k))
        o_copy(k).start()
    loop(1, S, send_rows)
    out[rows(g), fcols(s, c)] = finish(s)
    send_on(0)

    def arrive(k):
        place = region(source(k), g, c)
        copy(place, place, o_s.at[k], o_r.at[k], peer(k), t).wait_recv()
        send_on(k)
    loop(1, S, arrive)

    def arrive_y(k):
        def one(d):
            place = region(source(k), origin(d), c)
            copy(place, place, oy_s.at[k * G + d], oy_r.at[k * G + d], s, mate).wait_recv()
            oc_copy(k, d).start()
        loop(1, G, one)
    loop(0, S, arrive_y)

    def arrive_mate(k):
        def one(d):
            place = region(source(k), origin(d), 1 - c)
            copy(place, place, oc_s.at[k * G + d], oc_r.at[k * G + d], s, mate).wait_recv()
        loop(0, G, one)
    loop(0, S, arrive_mate)

    wm_copy().wait_send()
    dm_own().wait_send()
    al_copy(0, 1).wait_send()
    loop(1, G, lambda d: ag_copy(d).wait_send())

    def drain(k):
        inv_copy(k).wait_send()
        x_copy(k).wait_send()
        dm_copy(k).wait_send()
        xm_copy(k).wait_send()
        al_copy(k, 0).wait_send()
        al_copy(k, 1).wait_send()
        o_copy(k).wait_send()
    loop(1, S, drain)
    dy_copy(1).wait_send()

    def drain_dy(i):
        dy_copy(2 * i).wait_send()
        relay(2 * i).wait_send()
    loop(1, Z, drain_dy)

    def drain_all(k):
        def one(d):
            p_copy(k, d).wait_send()
            oy_copy(k, d).wait_send()
            oc_copy(k, d).wait_send()
        loop(1, G, one)
        oc_copy(k, 0).wait_send()
    loop(0, S, drain_all)


def solution(mesh):
    S, T = mesh.shape["section"], mesh.shape["tensor"]
    G = T // 2

    def per_device(layer_input, norm_gain, kv_weight, kv_cotangent):
        tok, width = layer_input.shape
        feats, cols = kv_weight.shape
        hf, R = feats // 2, tok // G
        dma = pltpu.SemaphoreType.DMA
        vmem = pl.BlockSpec(memory_space=pltpu.VMEM)
        V = pltpu.VMEM
        return tuple(pl.pallas_call(
            functools.partial(kernel, S, T),
            out_shape=(jax.ShapeDtypeStruct((feats, cols), F32), jax.ShapeDtypeStruct((tok, width), BF16)),
            in_specs=[vmem] * 4,
            out_specs=(vmem, vmem),
            scratch_shapes=[
                V((S, 8, tok), F32), V((S, tok, 128), F32), V((tok, 128), F32),
                V((S, tok, cols), BF16), V((S, tok, cols), BF16), V((hf, cols), BF16),
                V((S, tok, hf), BF16), V((S, tok, hf), BF16), V((S * tok, hf), BF16),
                V((S, tok, hf), F32), V((G, S, R, hf), F32),
                V((S, 2, S, tok), F32), V((G, S, tok), F32), V((S, tok), F32), V((S, R, hf), BF16),
                dma((S,)), dma((S,)), dma((S,)), dma((S,)), dma((S,)), dma((S,)), dma((1,)), dma((1,)),
                dma((S,)), dma((S,)), dma((S,)), dma((S,)), dma((S * G,)), dma((S * G,)),
                dma((S * 2,)), dma((S * 2,)), dma((G,)), dma((G,)), dma((S,)), dma((S,)),
                dma((S * G,)), dma((S * G,)), dma((S * G,)), dma((S * G,)),
            ],
            compiler_params=pltpu.CompilerParams(
                collective_id=0, has_side_effects=True, vmem_limit_bytes=56 * 1024 * 1024),
        )(layer_input, norm_gain.reshape(1, width), kv_weight, kv_cotangent))

    return jax.shard_map(
        per_device,
        mesh=mesh,
        in_specs=(P("section", None), P(), P("section", "tensor"), P("section", "tensor")),
        out_specs=(P("section", "tensor"), P("section", None)),
        check_vma=False,
    )
```

```python
import functools

import jax
import jax.numpy as jnp
from jax import lax
from jax.experimental import pallas as pl
from jax.experimental.pallas import tpu as pltpu
from jax.sharding import PartitionSpec as P

MESH = pl.DeviceIdType.MESH
F32 = jnp.float32
BF16 = jnp.bfloat16
NT = (((1,), (1,)), ((), ()))
TN = (((0,), (0,)), ((), ()))


def kernel(S, T, x_in, gain, w_in, dy_in, wg_out, out, invs, invcol, colbuf, dy, dym, wm, xo, xm, nrm, part,
           prcv, albuf, alf, fin, x, w, dyin, wg, ld, inv_s, inv_r, dy_s, dy_r, dm_s, dm_r, wm_s, wm_r, x_s, x_r,
           xm_s, xm_r, p_s, p_r, al_s, al_r, o_s, o_r, oy_s, oy_r, oc_s, oc_r):
    s = lax.axis_index("section")
    t = lax.axis_index("tensor")
    c = t % 2
    g = t // 2
    G = T // 2
    Z = S // 2
    mate = g * 2 + 1 - c
    tok, width = x.shape
    feats = w.shape[0]
    hf = feats // 2
    R = tok // G

    def copy(src, dst, ss, rs, sec, ten):
        return pltpu.make_async_remote_copy(
            src_ref=src, dst_ref=dst, send_sem=ss, recv_sem=rs,
            device_id={"section": sec, "tensor": ten}, device_id_type=MESH,
        )

    def loop(lo, hi, f):
        def body(k, carry):
            f(k)
            return carry
        lax.fori_loop(lo, hi, body, 0)

    def peer(k):
        return (s // 2 + k // 2) % Z * 2 + (s + k) % 2

    def source(k):
        return (s // 2 + Z - k // 2) % Z * 2 + (s + k) % 2

    def other(d):
        return (g + d) % G

    def origin(d):
        return (g + G - d) % G

    def fcols(sec, half):
        return pl.ds(pl.multiple_of(sec * feats + half * hf, hf), hf)

    def rows(gg):
        return pl.ds(pl.multiple_of(gg * R, R), R)

    barrier = pltpu.get_barrier_semaphore()

    def hello(sec, ten):
        pl.semaphore_signal(barrier, inc=1, device_id={"section": sec, "tensor": ten}, device_id_type=MESH)

    def place_of(j):
        return peer(j // T), (t + j) % T
    loop(1, S * T, lambda j: hello(*place_of(j)))

    loads = [pltpu.make_async_copy(a, b, ld.at[i])
             for i, (a, b) in enumerate(((x_in, x), (w_in, w), (dy_in, dyin)))]
    for load in loads:
        load.start()
    loads[0].wait()

    def squares(i, acc):
        v = x[:, pl.ds(pl.multiple_of(i * feats, feats), feats)].astype(F32)
        return acc + jnp.sum(v * v, axis=1, keepdims=True)
    total = lax.fori_loop(0, width // feats, squares, jnp.zeros((tok, 1), F32))
    inv_own = lax.rsqrt(total / width + 1e-05)
    invs[s] = jnp.transpose(jnp.broadcast_to(inv_own, (tok, 128)))[0:8]
    loads[1].wait()
    loads[2].wait()
    pl.semaphore_wait(barrier, S * T - 1)

    def wm_copy():
        half = pl.ds(pl.multiple_of((1 - c) * hf, hf), hf)
        return copy(w.at[half], wm, wm_s.at[0], wm_r.at[0], s, mate)

    def dy_copy(k):
        return copy(dyin, dy.at[s], dy_s.at[k], dy_r.at[k], peer(k), t)

    def inv_copy(k):
        return copy(invs.at[s], invs.at[s], inv_s.at[k], inv_r.at[k], peer(k), t)

    def x_copy(k):
        return copy(x.at[:, fcols(peer(k), c)], xo.at[s], x_s.at[k], x_r.at[k], peer(k), t)

    def dm_copy(k):
        return copy(dy.at[source(k)], dym.at[source(k)], dm_s.at[k], dm_r.at[k], s, mate)

    def dm_own():
        return copy(dyin, dym.at[s], dm_s.at[0], dm_r.at[0], s, mate)

    def xm_copy(k):
        return copy(xo.at[source(k)], xm.at[source(k)], xm_s.at[k], xm_r.at[k], s, mate)

    wm_copy().start()
    dm_own().start()
    dy_copy(1).start()
    loop(1, Z, lambda i: dy_copy(2 * i).start())
    loop(1, S, lambda k: inv_copy(k).start())
    loop(1, Z, lambda i: x_copy(2 * i).start())
    dy[s] = dyin[...]
    xo[s] = x[:, fcols(s, c)]
    xm[s] = x[:, fcols(s, 1 - c)]

    wm_copy().wait_recv()
    own_half = pl.ds(pl.multiple_of(c * hf, hf), hf)

    def p_copy(k, d):
        sec = source(k)
        i = k * G + d
        return copy(part.at[sec, rows(other(d))], prcv.at[d, sec], p_s.at[i], p_r.at[i], s, other(d) * 2 + c)

    def multiply(k):
        sec = source(k)
        dm_copy(k).wait_recv()
        part[sec] = lax.dot_general(dy[sec], w[own_half, :], NT, preferred_element_type=F32) + lax.dot_general(
            dym[sec], wm[...], NT, preferred_element_type=F32)

    def pass_cotangent(k):
        copy(dyin, dy.at[source(k)], dy_s.at[k], dy_r.at[k], peer(k), t).wait_recv()
        dm_copy(k).start()

    def relay(k):
        return copy(dy.at[source(k)], dy.at[source(k)], dy_s.at[k + 1], dy_r.at[k + 1], peer(1), t)

    def pass_relay(k):
        pass_cotangent(k)
        relay(k).start()

    def use(k):
        multiply(k)
        loop(1, G, lambda d: p_copy(k, d).start())

    pass_cotangent(1)
    use(0)
    pass_relay(2)
    use(1)

    def even(i):
        pass_relay(2 * i)
        use(2 * i - 2)
    loop(2, Z, even)
    loop(0, Z, lambda i: x_copy(2 * i + 1).start())
    use(2 * Z - 2)
    pass_cotangent(3)

    def odd(i):
        pass_cotangent(2 * i + 1)
        use(2 * i - 1)
    loop(2, Z, odd)
    use(2 * Z - 1)

    lanes = lax.broadcasted_iota(jnp.int32, (S, tok), 0)

    def unit_block(k, acc):
        sec = source(k)
        col = jnp.transpose(jnp.broadcast_to(invs[sec][0:1], (128, tok)))
        invcol[sec] = col
        unit = xo[sec].astype(F32) * col[:, 0:1]
        scaled = unit * gain[:, fcols(s, c)]
        nrm[pl.ds(pl.multiple_of(sec * tok, tok), tok), :] = scaled.astype(BF16)
        sums = jnp.sum(scaled * part[sec], axis=1, keepdims=True)
        row = jnp.transpose(jnp.broadcast_to(sums, (tok, 128)))[0:1]
        return jnp.where(lanes == sec, jnp.broadcast_to(row, (S, tok)), acc)

    def token_block(k, acc):
        sec = source(k)
        copy(invs.at[s], invs.at[sec], inv_s.at[k], inv_r.at[k], peer(k), t).wait_recv()
        copy(xo.at[s], xo.at[sec], x_s.at[k], x_r.at[k], peer(k), t).wait_recv()
        xm_copy(k).start()
        return unit_block(k, acc)

    def grad_block(k, first=False):
        sec = source(k)
        if not first:
            xm_copy(k).wait_recv()
        unit = xm[sec].astype(F32) * invcol[sec][:, 0:1]
        scaled = (unit * gain[:, fcols(s, 1 - c)]).astype(BF16)
        own = nrm[pl.ds(pl.multiple_of(sec * tok, tok), tok), :]
        for half, block in ((c, own), (1 - c, scaled)):
            place = pl.ds(pl.multiple_of(half * hf, hf), hf)
            term = lax.dot_general(block, dy[sec], TN, preferred_element_type=F32)
            wg[place, :] = term if first else wg[place, :] + term

    along = unit_block(0, jnp.zeros((S, tok), F32))
    along = token_block(2, along)
    grad_block(0, True)

    def even_block(i, acc):
        acc = token_block(2 * i, acc)
        grad_block(2 * i - 2)
        return acc

    def odd_block(i, acc):
        acc = token_block(2 * i + 1, acc)
        grad_block(2 * i - 1)
        return acc
    along = lax.fori_loop(2, Z, even_block, along)
    along = token_block(1, along)
    grad_block(2 * Z - 2)
    along = lax.fori_loop(1, Z, odd_block, along)
    albuf[0] = along

    def al_copy(j):
        sec, ten = place_of(j)
        return copy(albuf.at[0], albuf.at[j], al_s.at[j], al_r.at[j], sec, ten)
    loop(1, S * T, lambda j: al_copy(j).start())

    grad_block(2 * Z - 1)
    store = pltpu.make_async_copy(wg, wg_out, ld.at[3])
    store.start()

    def p_wait(k):
        loop(1, G, lambda d: p_copy(k, d).wait_recv())
    loop(0, S, p_wait)

    def al_wait(j, acc):
        al_copy(j).wait_recv()
        return acc + albuf[j]
    alf[...] = lax.fori_loop(1, S * T, al_wait, along) / width

    def finish(sec):
        def add(d, acc):
            return acc + prcv[d, sec]
        reduced = lax.fori_loop(1, G, add, part[sec, rows(g), :])
        colbuf[...] = jnp.transpose(jnp.broadcast_to(alf[pl.ds(sec, 1), :], (128, tok)))
        inv = invcol[sec, rows(g), :][:, 0:1]
        al = colbuf[rows(g), :][:, 0:1]
        unit = xo[sec, rows(g), :].astype(F32) * inv
        return (inv * (gain[:, fcols(s, c)] * reduced - unit * al)).astype(BF16)

    def region(sec, gg, half):
        return out.at[rows(gg), fcols(sec, half)]

    def o_copy(k):
        return copy(fin.at[peer(k)], region(s, g, c), o_s.at[k], o_r.at[k], peer(k), t)

    def oy_copy(k, d):
        place = region(source(k), g, c)
        return copy(place, place, oy_s.at[k * G + d], oy_r.at[k * G + d], s, other(d) * 2 + c)

    def oc_copy(k, d):
        place = region(source(k), origin(d), c)
        return copy(place, place, oc_s.at[k * G + d], oc_r.at[k * G + d], s, mate)

    def send_on(k):
        loop(1, G, lambda d: oy_copy(k, d).start())
        oc_copy(k, 0).start()

    def send_rows(k):
        fin[peer(k)] = finish(peer(k))
        o_copy(k).start()
    loop(1, S, send_rows)
    out[rows(g), fcols(s, c)] = finish(s)
    send_on(0)

    def arrive(k):
        place = region(source(k), g, c)
        copy(place, place, o_s.at[k], o_r.at[k], peer(k), t).wait_recv()
        send_on(k)
    loop(1, S, arrive)

    def arrive_y(k):
        def one(d):
            place = region(source(k), origin(d), c)
            copy(place, place, oy_s.at[k * G + d], oy_r.at[k * G + d], s, mate).wait_recv()
            oc_copy(k, d).start()
        loop(1, G, one)
    loop(0, S, arrive_y)

    def arrive_mate(k):
        def one(d):
            place = region(source(k), origin(d), 1 - c)
            copy(place, place, oc_s.at[k * G + d], oc_r.at[k * G + d], s, mate).wait_recv()
        loop(0, G, one)
    loop(0, S, arrive_mate)

    wm_copy().wait_send()
    dm_own().wait_send()
    loop(1, S * T, lambda j: al_copy(j).wait_send())
    store.wait()

    def drain(k):
        inv_copy(k).wait_send()
        x_copy(k).wait_send()
        dm_copy(k).wait_send()
        xm_copy(k).wait_send()
        o_copy(k).wait_send()
    loop(1, S, drain)
    dy_copy(1).wait_send()

    def drain_dy(i):
        dy_copy(2 * i).wait_send()
        relay(2 * i).wait_send()
    loop(1, Z, drain_dy)

    def drain_all(k):
        def one(d):
            p_copy(k, d).wait_send()
            oy_copy(k, d).wait_send()
            oc_copy(k, d).wait_send()
        loop(1, G, one)
        oc_copy(k, 0).wait_send()
    loop(0, S, drain_all)


def solution(mesh):
    S, T = mesh.shape["section"], mesh.shape["tensor"]
    G = T // 2

    def per_device(layer_input, norm_gain, kv_weight, kv_cotangent):
        tok, width = layer_input.shape
        feats, cols = kv_weight.shape
        hf, R = feats // 2, tok // G
        dma = pltpu.SemaphoreType.DMA
        vmem = pl.BlockSpec(memory_space=pltpu.VMEM)
        hbm = pl.BlockSpec(memory_space=pl.ANY)
        V = pltpu.VMEM
        return tuple(pl.pallas_call(
            functools.partial(kernel, S, T),
            out_shape=(jax.ShapeDtypeStruct((feats, cols), F32), jax.ShapeDtypeStruct((tok, width), BF16)),
            in_specs=[hbm, vmem, hbm, hbm],
            out_specs=(hbm, vmem),
            scratch_shapes=[
                V((S, 8, tok), F32), V((S, tok, 128), F32), V((tok, 128), F32),
                V((S, tok, cols), BF16), V((S, tok, cols), BF16), V((hf, cols), BF16),
                V((S, tok, hf), BF16), V((S, tok, hf), BF16), V((S * tok, hf), BF16),
                V((S, tok, hf), F32), V((G, S, R, hf), F32),
                V((S * T, S, tok), F32), V((S, tok), F32), V((S, R, hf), BF16),
                V((tok, width), BF16), V((feats, cols), BF16), V((tok, cols), BF16), V((feats, cols), F32), dma((4,)),
                dma((S,)), dma((S,)), dma((S,)), dma((S,)), dma((S,)), dma((S,)), dma((1,)), dma((1,)),
                dma((S,)), dma((S,)), dma((S,)), dma((S,)), dma((S * G,)), dma((S * G,)),
                dma((S * T,)), dma((S * T,)), dma((S,)), dma((S,)),
                dma((S * G,)), dma((S * G,)), dma((S * G,)), dma((S * G,)),
            ],
            compiler_params=pltpu.CompilerParams(
                collective_id=0, has_side_effects=True, vmem_limit_bytes=56 * 1024 * 1024),
        )(layer_input, norm_gain.reshape(1, width), kv_weight, kv_cotangent))

    return jax.shard_map(
        per_device,
        mesh=mesh,
        in_specs=(P("section", None), P(), P("section", "tensor"), P("section", "tensor")),
        out_specs=(P("section", "tensor"), P("section", None)),
        check_vma=False,
    )
```

```python
import functools

import jax
import jax.numpy as jnp
from jax import lax
from jax.experimental import pallas as pl
from jax.experimental.pallas import tpu as pltpu
from jax.sharding import PartitionSpec as P

MESH = pl.DeviceIdType.MESH
F32 = jnp.float32
BF16 = jnp.bfloat16
NT = (((1,), (1,)), ((), ()))
TN = (((0,), (0,)), ((), ()))


def kernel(S, T, x, gain, w, dyin, wg, out, invs, invcol, colbuf, dy, dym, wm, xo, xm, nrm, part,
           prcv, albuf, agbuf, alf, fin, inv_s, inv_r, dy_s, dy_r, dm_s, dm_r, wm_s, wm_r, x_s, x_r,
           xm_s, xm_r, p_s, p_r, al_s, al_r, ag_s, ag_r, o_s, o_r, oy_s, oy_r, oc_s, oc_r):
    s = lax.axis_index("section")
    t = lax.axis_index("tensor")
    c = t % 2
    g = t // 2
    G = T // 2
    Z = S // 2
    mate = g * 2 + 1 - c
    tok, width = x.shape
    feats = w.shape[0]
    hf = feats // 2
    R = tok // G

    def copy(src, dst, ss, rs, sec, ten):
        return pltpu.make_async_remote_copy(
            src_ref=src, dst_ref=dst, send_sem=ss, recv_sem=rs,
            device_id={"section": sec, "tensor": ten}, device_id_type=MESH,
        )

    def loop(lo, hi, f):
        def body(k, carry):
            f(k)
            return carry
        lax.fori_loop(lo, hi, body, 0)

    def peer(k):
        return (s // 2 + k // 2) % Z * 2 + (s + k) % 2

    def source(k):
        return (s // 2 + Z - k // 2) % Z * 2 + (s + k) % 2

    def other(d):
        return (g + d) % G

    def origin(d):
        return (g + G - d) % G

    def fcols(sec, half):
        return pl.ds(pl.multiple_of(sec * feats + half * hf, hf), hf)

    def rows(gg):
        return pl.ds(pl.multiple_of(gg * R, R), R)

    barrier = pltpu.get_barrier_semaphore()

    def hello(sec, ten):
        pl.semaphore_signal(barrier, inc=1, device_id={"section": sec, "tensor": ten}, device_id_type=MESH)

    def greet(k):
        hello(peer(k), t)
        hello(peer(k), mate)
    loop(1, S, greet)
    hello(s, mate)
    loop(1, G, lambda d: hello(s, other(d) * 2 + c))

    def squares(i, acc):
        v = x[:, pl.ds(pl.multiple_of(i * feats, feats), feats)].astype(F32)
        return acc + jnp.sum(v * v, axis=1, keepdims=True)
    total = lax.fori_loop(0, width // feats, squares, jnp.zeros((tok, 1), F32))
    inv_own = lax.rsqrt(total / width + 1e-05)
    invs[s] = jnp.transpose(jnp.broadcast_to(inv_own, (tok, 128)))[0:8]
    pl.semaphore_wait(barrier, 2 * S - 1 + G - 1)

    def wm_copy():
        half = pl.ds(pl.multiple_of((1 - c) * hf, hf), hf)
        return copy(w.at[half], wm, wm_s.at[0], wm_r.at[0], s, mate)

    def dy_copy(k):
        return copy(dyin, dy.at[s], dy_s.at[k], dy_r.at[k], peer(k), t)

    def inv_copy(k):
        return copy(invs.at[s], invs.at[s], inv_s.at[k], inv_r.at[k], peer(k), t)

    def x_copy(k):
        return copy(x.at[:, fcols(peer(k), c)], xo.at[s], x_s.at[k], x_r.at[k], peer(k), t)

    def dm_copy(k):
        return copy(dy.at[source(k)], dym.at[source(k)], dm_s.at[k], dm_r.at[k], s, mate)

    def dm_own():
        return copy(dyin, dym.at[s], dm_s.at[0], dm_r.at[0], s, mate)

    def xm_copy(k):
        return copy(xo.at[source(k)], xm.at[source(k)], xm_s.at[k], xm_r.at[k], s, mate)

    wm_copy().start()
    dm_own().start()
    dy_copy(1).start()
    loop(1, Z, lambda i: dy_copy(2 * i).start())
    loop(1, S, lambda k: inv_copy(k).start())
    loop(1, Z, lambda i: x_copy(2 * i).start())
    dy[s] = dyin[...]
    xo[s] = x[:, fcols(s, c)]
    xm[s] = x[:, fcols(s, 1 - c)]

    wm_copy().wait_recv()
    own_half = pl.ds(pl.multiple_of(c * hf, hf), hf)

    def p_copy(k, d):
        sec = source(k)
        i = k * G + d
        return copy(part.at[sec, rows(other(d))], prcv.at[d, sec], p_s.at[i], p_r.at[i], s, other(d) * 2 + c)

    def multiply(k):
        sec = source(k)
        dm_copy(k).wait_recv()
        part[sec] = lax.dot_general(dy[sec], w[own_half, :], NT, preferred_element_type=F32) + lax.dot_general(
            dym[sec], wm[...], NT, preferred_element_type=F32)

    def pass_cotangent(k):
        copy(dyin, dy.at[source(k)], dy_s.at[k], dy_r.at[k], peer(k), t).wait_recv()
        dm_copy(k).start()

    def relay(k):
        return copy(dy.at[source(k)], dy.at[source(k)], dy_s.at[k + 1], dy_r.at[k + 1], peer(1), t)

    def pass_relay(k):
        pass_cotangent(k)
        relay(k).start()

    def use(k):
        multiply(k)
        loop(1, G, lambda d: p_copy(k, d).start())

    pass_cotangent(1)
    use(0)
    pass_relay(2)
    use(1)

    def even(i):
        pass_relay(2 * i)
        use(2 * i - 2)
    loop(2, Z, even)
    loop(0, Z, lambda i: x_copy(2 * i + 1).start())
    use(2 * Z - 2)
    pass_cotangent(3)

    def odd(i):
        pass_cotangent(2 * i + 1)
        use(2 * i - 1)
    loop(2, Z, odd)
    use(2 * Z - 1)

    lanes = lax.broadcasted_iota(jnp.int32, (S, tok), 0)

    def unit_block(k, acc):
        sec = source(k)
        col = jnp.transpose(jnp.broadcast_to(invs[sec][0:1], (128, tok)))
        invcol[sec] = col
        unit = xo[sec].astype(F32) * col[:, 0:1]
        scaled = unit * gain[:, fcols(s, c)]
        nrm[pl.ds(pl.multiple_of(sec * tok, tok), tok), :] = scaled.astype(BF16)
        sums = jnp.sum(scaled * part[sec], axis=1, keepdims=True)
        row = jnp.transpose(jnp.broadcast_to(sums, (tok, 128)))[0:1]
        return jnp.where(lanes == sec, jnp.broadcast_to(row, (S, tok)), acc)

    def token_block(k, acc):
        sec = source(k)
        copy(invs.at[s], invs.at[sec], inv_s.at[k], inv_r.at[k], peer(k), t).wait_recv()
        copy(xo.at[s], xo.at[sec], x_s.at[k], x_r.at[k], peer(k), t).wait_recv()
        xm_copy(k).start()
        return unit_block(k, acc)
    along = unit_block(0, jnp.zeros((S, tok), F32))
    along = lax.fori_loop(1, Z, lambda i, acc: token_block(2 * i, acc), along)
    along = lax.fori_loop(0, Z, lambda i, acc: token_block(2 * i + 1, acc), along)
    albuf[0, 0] = along

    def al_copy(k, m):
        return copy(albuf.at[0, 0], albuf.at[k, m], al_s.at[k * 2 + m], al_r.at[k * 2 + m], peer(k),
                    t if m == 0 else mate)

    def al_send(k):
        al_copy(k, 0).start()
        al_copy(k, 1).start()
    al_copy(0, 1).start()
    loop(1, S, al_send)

    def weight_half(half):
        flat = dy[...].reshape(S * tok, dyin.shape[1])
        wg[pl.ds(pl.multiple_of(half * hf, hf), hf), :] = lax.dot_general(
            nrm[...], flat, TN, preferred_element_type=F32)
    weight_half(c)

    al_copy(0, 1).wait_recv()

    def al_wait(k, acc):
        al_copy(k, 0).wait_recv()
        al_copy(k, 1).wait_recv()
        return acc + (albuf[k, 0] + albuf[k, 1])
    along = lax.fori_loop(1, S, al_wait, albuf[0, 0] + albuf[0, 1])
    agbuf[0] = along

    def ag_copy(d):
        return copy(agbuf.at[0], agbuf.at[d], ag_s.at[d], ag_r.at[d], s, other(d) * 2 + c)
    loop(1, G, lambda d: ag_copy(d).start())

    def ag_wait(d, acc):
        ag_copy(d).wait_recv()
        return acc + agbuf[d]

    def p_wait(k):
        loop(1, G, lambda d: p_copy(k, d).wait_recv())
    loop(0, S, p_wait)
    alf[...] = lax.fori_loop(1, G, ag_wait, along) / width

    def finish(sec):
        def add(d, acc):
            return acc + prcv[d, sec]
        reduced = lax.fori_loop(1, G, add, part[sec, rows(g), :])
        colbuf[...] = jnp.transpose(jnp.broadcast_to(alf[pl.ds(sec, 1), :], (128, tok)))
        inv = invcol[sec, rows(g), :][:, 0:1]
        al = colbuf[rows(g), :][:, 0:1]
        unit = xo[sec, rows(g), :].astype(F32) * inv
        return (inv * (gain[:, fcols(s, c)] * reduced - unit * al)).astype(BF16)

    def region(sec, gg, half):
        return out.at[rows(gg), fcols(sec, half)]

    def o_copy(k):
        return copy(fin.at[peer(k)], region(s, g, c), o_s.at[k], o_r.at[k], peer(k), t)

    def oy_copy(k, d):
        place = region(source(k), g, c)
        return copy(place, place, oy_s.at[k * G + d], oy_r.at[k * G + d], s, other(d) * 2 + c)

    def oc_copy(k, d):
        place = region(source(k), origin(d), c)
        return copy(place, place, oc_s.at[k * G + d], oc_r.at[k * G + d], s, mate)

    def send_on(k):
        loop(1, G, lambda d: oy_copy(k, d).start())
        oc_copy(k, 0).start()

    def send_rows(k):
        fin[peer(k)] = finish(peer(k))
        o_copy(k).start()
    out[rows(g), fcols(s, c)] = finish(s)
    send_on(0)
    loop(1, S, send_rows)

    def mate_block(k):
        sec = source(k)
        unit = xm[sec].astype(F32) * invcol[sec][:, 0:1]
        scaled = unit * gain[:, fcols(s, 1 - c)]
        nrm[pl.ds(pl.multiple_of(sec * tok, tok), tok), :] = scaled.astype(BF16)

    def mate_wait(k):
        xm_copy(k).wait_recv()
        mate_block(k)
    mate_block(0)
    loop(1, S, mate_wait)
    weight_half(1 - c)

    def arrive(k):
        place = region(source(k), g, c)
        copy(place, place, o_s.at[k], o_r.at[k], peer(k), t).wait_recv()
        send_on(k)
    loop(1, S, arrive)

    def arrive_y(k):
        def one(d):
            place = region(source(k), origin(d), c)
            copy(place, place, oy_s.at[k * G + d], oy_r.at[k * G + d], s, mate).wait_recv()
            oc_copy(k, d).start()
        loop(1, G, one)
    loop(0, S, arrive_y)

    def arrive_mate(k):
        def one(d):
            place = region(source(k), origin(d), 1 - c)
            copy(place, place, oc_s.at[k * G + d], oc_r.at[k * G + d], s, mate).wait_recv()
        loop(0, G, one)
    loop(0, S, arrive_mate)

    wm_copy().wait_send()
    dm_own().wait_send()
    al_copy(0, 1).wait_send()
    loop(1, G, lambda d: ag_copy(d).wait_send())

    def drain(k):
        inv_copy(k).wait_send()
        x_copy(k).wait_send()
        dm_copy(k).wait_send()
        xm_copy(k).wait_send()
        al_copy(k, 0).wait_send()
        al_copy(k, 1).wait_send()
        o_copy(k).wait_send()
    loop(1, S, drain)
    dy_copy(1).wait_send()

    def drain_dy(i):
        dy_copy(2 * i).wait_send()
        relay(2 * i).wait_send()
    loop(1, Z, drain_dy)

    def drain_all(k):
        def one(d):
            p_copy(k, d).wait_send()
            oy_copy(k, d).wait_send()
            oc_copy(k, d).wait_send()
        loop(1, G, one)
        oc_copy(k, 0).wait_send()
    loop(0, S, drain_all)


def solution(mesh):
    S, T = mesh.shape["section"], mesh.shape["tensor"]
    G = T // 2

    def per_device(layer_input, norm_gain, kv_weight, kv_cotangent):
        tok, width = layer_input.shape
        feats, cols = kv_weight.shape
        hf, R = feats // 2, tok // G
        dma = pltpu.SemaphoreType.DMA
        vmem = pl.BlockSpec(memory_space=pltpu.VMEM)
        V = pltpu.VMEM
        return tuple(pl.pallas_call(
            functools.partial(kernel, S, T),
            out_shape=(jax.ShapeDtypeStruct((feats, cols), F32), jax.ShapeDtypeStruct((tok, width), BF16)),
            in_specs=[vmem] * 4,
            out_specs=(vmem, vmem),
            scratch_shapes=[
                V((S, 8, tok), F32), V((S, tok, 128), F32), V((tok, 128), F32),
                V((S, tok, cols), BF16), V((S, tok, cols), BF16), V((hf, cols), BF16),
                V((S, tok, hf), BF16), V((S, tok, hf), BF16), V((S * tok, hf), BF16),
                V((S, tok, hf), F32), V((G, S, R, hf), F32),
                V((S, 2, S, tok), F32), V((G, S, tok), F32), V((S, tok), F32), V((S, R, hf), BF16),
                dma((S,)), dma((S,)), dma((S,)), dma((S,)), dma((S,)), dma((S,)), dma((1,)), dma((1,)),
                dma((S,)), dma((S,)), dma((S,)), dma((S,)), dma((S * G,)), dma((S * G,)),
                dma((S * 2,)), dma((S * 2,)), dma((G,)), dma((G,)), dma((S,)), dma((S,)),
                dma((S * G,)), dma((S * G,)), dma((S * G,)), dma((S * G,)),
            ],
            compiler_params=pltpu.CompilerParams(
                collective_id=0, has_side_effects=True, vmem_limit_bytes=56 * 1024 * 1024),
        )(layer_input, norm_gain.reshape(1, width), kv_weight, kv_cotangent))

    return jax.shard_map(
        per_device,
        mesh=mesh,
        in_specs=(P("section", None), P(), P("section", "tensor"), P("section", "tensor")),
        out_specs=(P("section", "tensor"), P("section", None)),
        check_vma=False,
    )
```
